256 devices in a mesh: lat: 128 (over z, y, x), field: 2 (over core).
Axes of the slice: x: 4, y: 4, z: 8, core: 2. Of those that a mesh axis runs over, the one named last changes fastest.
Arguments:
- fields_grid: bfloat16 [2, 64, 2, 384, 1536], P('field', None, None, 'lat'), may hold values from -6 to 6
- basis: bfloat16 [1024, 384, 768], P('lat'), may hold values from -0.3125 to 0.3125
- order_table: int32 [128, 8], replicated, may hold values from -1 to 767, as said below
- panel_modes: int32 [2, 64], replicated, may hold values from 0 to 767, as said below
Outputs:
- panel: bfloat16 [2, 1024, 1536, 128], P('field', 'lat')
The draws below stay inside these ranges and needn't reach their ends.
Inputs may be any that keep to these rules, and one draw needn't show every extreme that they name: `order_table`: each order 0 to 767 stands in exactly one slot; every other slot holds -1; some group has all 8 slots filled. `panel_modes`: row 1 is never smaller than row 0 in the same column; degree 767 appears.
All inputs are finite; a program needn't handle non-finite values.
Results may differ from the reference program's by a relative error of at most 0.0082.
Values may be sent and summed in bfloat16 or wider, within the bound.
No kernel may reach another device: no remote copies, remote signals or barrier semaphores. Data moves between devices by JAX's collectives and lax.ppermute only.
A program may use at most 64 MiB of HBM per device.

```python
import math
import jax
import jax.numpy as jnp
from jax import lax

SLOTS = 8
SNAP = 64
NMODE = 64
GROUPS = 128
NPAIR = 384
NLON = 1536
NORD = 768
LDEG = 768


def draw_order_table(key, part):
    total = GROUPS * SLOTS
    first_key, second_key, third_key = jax.random.split(key, 3)
    full_group = jax.random.randint(first_key, (), 0, GROUPS)
    positions = jax.random.permutation(second_key, total)
    priority = jnp.where(positions // SLOTS == full_group, 0, 1).astype(jnp.int32)
    ordered = positions[jnp.argsort(priority, stable=True)]
    orders = jax.random.permutation(third_key, NORD).astype(jnp.int32)
    flat_table = jnp.full((total,), -1, dtype=jnp.int32).at[ordered[:NORD]].set(orders)
    return flat_table.reshape(GROUPS, SLOTS).astype(jnp.int32)


def draw_panel_modes(key, part):
    first_key, second_key = jax.random.split(key)
    mode_order = jax.random.randint(first_key, (NMODE,), 0, NORD).astype(jnp.int32)
    offset = jax.random.randint(second_key, (NMODE,), 0, LDEG - mode_order).astype(jnp.int32)
    degree = mode_order + offset
    mode_order = mode_order.at[0].set(0).at[1].set(NORD - 1)
    degree = degree.at[0].set(NORD - 1).at[1].set(NORD - 1)
    return jnp.stack([mode_order, degree]).astype(jnp.int32)


def levels(stream_key, extent, cuts, least, top_value):
    def one(axis_at, blocks):
        draws = jax.random.uniform(jax.random.fold_in(jax.random.fold_in(stream_key, 6), axis_at), (blocks,), jnp.float32, least / len(cuts), top_value / len(cuts))
        return jnp.repeat(jnp.exp(draws), extent[axis_at] // blocks).reshape((-1,) + (1,) * (len(extent) - axis_at - 1))

    gain = one(*cuts[0])
    for cut in cuts[1:]:
        gain = gain * one(*cut)
    return gain


def gaussian(stream_key, extent, width, bound, shards=(), kind=jnp.bfloat16):
    loudness = levels(stream_key, extent, shards, -0.22, 0.18) if shards else 1.0
    values = jax.random.normal(stream_key, extent, jnp.float32) * width * loudness
    return jnp.minimum(jnp.maximum(values, -bound), bound).astype(kind)


def setup_inputs(seed: int = 0) -> dict:
    keys = jax.random.split(jax.random.key(seed), 5)
    fields_grid = gaussian(keys[0], (2, SNAP, 2, NPAIR, NLON), 1.0, 6.0, ((0, 2), (3, 128)))
    basis = gaussian(keys[1], (GROUPS * SLOTS, NPAIR, LDEG), NPAIR ** -0.5, 0.3125, ((0, 128),))
    order_table = draw_order_table(jax.random.fold_in(keys[4], 71), 0)
    panel_modes = draw_panel_modes(jax.random.fold_in(keys[4], 71), 0)
    return {"fields_grid": fields_grid, "basis": basis, "order_table": order_table, "panel_modes": panel_modes}


def dft_table(orders, lon_count):
    valid_slot = orders >= 0
    safe_orders = jnp.maximum(orders, 0).astype(jnp.int32)
    products = jnp.arange(lon_count, dtype=jnp.int32)[:, None] * safe_orders[None, :] % lon_count
    angles = products.astype(jnp.float32) * (2.0 * math.pi / lon_count)
    cosine = jnp.where(valid_slot[None, :], jnp.cos(angles), 0.0).astype(jnp.bfloat16)
    sine_table = jnp.where(valid_slot[None, :], -jnp.sin(angles), 0.0).astype(jnp.bfloat16)
    return jnp.stack([cosine, sine_table], axis=1)

def field_coefficients(grid_one, basis, orders, dft):
    snap_count = grid_one.shape[0]
    slot_all = orders.shape[0]
    fourier = jnp.einsum('thjn,nrk->hkjrt', grid_one, dft, preferred_element_type=jnp.float32) * (1.0 / math.sqrt(NLON))
    fourier = fourier.reshape(2, slot_all, NPAIR, 2 * snap_count)
    parity_parts = jnp.stack([fourier[0] + fourier[1], fourier[0] - fourier[1]]).astype(jnp.bfloat16)
    degree = jnp.arange(LDEG, dtype=jnp.int32)

    def one_group(index):
        start = (index * SLOTS).astype(jnp.int32)
        basis_block = lax.dynamic_slice_in_dim(basis, start, SLOTS, 0).astype(jnp.float32)
        even_block = lax.dynamic_slice_in_dim(parity_parts[0], start, SLOTS, 0).astype(jnp.float32)
        odd_block = lax.dynamic_slice_in_dim(parity_parts[1], start, SLOTS, 0).astype(jnp.float32)
        group_orders = lax.dynamic_slice_in_dim(orders, start, SLOTS, 0)
        even_product = jnp.einsum('sjl,sjc->slc', basis_block, even_block)
        odd_product = jnp.einsum('sjl,sjc->slc', basis_block, odd_block)
        parity_odd = (degree[None, :] - group_orders[:, None]) % 2 == 1
        chosen = jnp.where(parity_odd[:, :, None], odd_product, even_product)
        keep_mask = (degree[None, :] >= group_orders[:, None]) & (group_orders >= 0)[:, None]
        return jnp.where(keep_mask[:, :, None], chosen, 0.0).astype(jnp.bfloat16)
    blocks = lax.map(one_group, jnp.arange(slot_all // SLOTS, dtype=jnp.int32))
    return blocks.reshape(slot_all, LDEG, 2 * snap_count)

def reference(fields_grid, basis, order_table, panel_modes):
    snap_count = fields_grid.shape[1]
    orders = order_table.reshape(-1).astype(jnp.int32)
    slot_all = orders.shape[0]
    dft = dft_table(orders, NLON)
    coefficients = lax.map(lambda grid_one: field_coefficients(grid_one, basis, orders, dft), fields_grid)
    mode_order = panel_modes[0].astype(jnp.int32)
    mode_degree = panel_modes[1].astype(jnp.int32)
    slot_of_mode = jnp.argmax(orders[None, :] == mode_order[:, None], axis=1).astype(jnp.int32)
    mode_values = coefficients[:, slot_of_mode, mode_degree, :]
    columns = mode_values.astype(jnp.float32).reshape(2, NMODE * 2, snap_count)
    centered = (columns - lax.optimization_barrier(jnp.mean(columns, axis=2, keepdims=True))).astype(jnp.bfloat16)
    scale = 1.0 / (snap_count - 1)

    def one_field(index):
        own = coefficients[index]
        partner = centered[1 - index]

        def one_group(group):
            start = (group * SLOTS).astype(jnp.int32)
            block = lax.dynamic_slice_in_dim(own, start, SLOTS, 0).reshape(SLOTS * LDEG * 2, snap_count)
            values = jnp.dot(block, partner.T, preferred_element_type=jnp.float32) * scale
            return values.astype(jnp.bfloat16).reshape(SLOTS, 2 * LDEG, 2 * NMODE)
        return lax.map(one_group, jnp.arange(slot_all // SLOTS, dtype=jnp.int32)).reshape(slot_all, 2 * LDEG, 2 * NMODE)
    return lax.map(one_field, jnp.arange(2, dtype=jnp.int32))
```

```python
import math

import jax
import jax.numpy as jnp
import numpy as np
from jax import lax
from jax.sharding import PartitionSpec as P


def dft_table(lon_count, order_count):
    products = np.arange(lon_count)[:, None] * np.arange(order_count)[None, :] % lon_count
    angles = products * (2.0 * math.pi / lon_count)
    return np.stack([np.cos(angles), -np.sin(angles)], axis=1).astype(jnp.bfloat16)


def doubled(block, axis):
    count = lax.axis_size(axis)
    reach = 1
    while reach < count:
        block = block + lax.ppermute(block, axis, [(i, i ^ reach) for i in range(count)])
        reach *= 2
    return block


def local(fields_grid, basis, order_table, panel_modes):
    grid_one = fields_grid[0]
    snap_count, _, pair_count, lon_count = grid_one.shape
    group_count, slot_count = order_table.shape
    pair_total, deg_count = basis.shape[1], basis.shape[2]
    mode_count = panel_modes.shape[1]
    order_count = lon_count // 2
    orders = order_table.reshape(-1)
    slot_all = orders.shape[0]

    table = jnp.asarray(dft_table(lon_count, order_count))
    fourier = jnp.einsum("thjn,nrm->hjrtm", grid_one, table, preferred_element_type=jnp.float32)
    fourier = fourier * (1.0 / math.sqrt(lon_count))
    parts = jnp.stack([fourier[0] + fourier[1], fourier[0] - fourier[1]]).astype(jnp.bfloat16)
    parts = parts.reshape(2 * pair_count * 2 * snap_count, order_count)
    placed = (orders[:, None] == lax.broadcasted_iota(jnp.int32, (1, order_count), 1)).astype(
        jnp.bfloat16
    )
    sent = lax.dot_general(
        placed, parts, (((1,), (1,)), ((), ())), preferred_element_type=jnp.float32
    ).astype(jnp.bfloat16)
    sent = sent.reshape(group_count, slot_count * 2 * pair_count, 2 * snap_count)
    received = lax.all_to_all(sent, "lat", split_axis=0, concat_axis=0, tiled=True)
    received = received.reshape(group_count, slot_count, 2, pair_count, 2 * snap_count)

    group_index = lax.axis_index("lat")
    my_orders = lax.dynamic_slice_in_dim(order_table, group_index, 1, 0)[0]
    rows = received.transpose(1, 0, 3, 2, 4).reshape(slot_count, pair_total, 4 * snap_count)
    both = jnp.einsum("sjl,sjc->slc", basis, rows, preferred_element_type=jnp.float32)
    degree = lax.broadcasted_iota(jnp.int32, (1, deg_count), 1)
    odd = (degree - my_orders[:, None]) % 2 == 1
    keep = (degree >= my_orders[:, None]) & (my_orders >= 0)[:, None]
    chosen = jnp.where(odd[:, :, None], both[:, :, 2 * snap_count :], both[:, :, : 2 * snap_count])
    coefficients = jnp.where(keep[:, :, None], chosen, 0.0).astype(jnp.bfloat16)

    owned = (my_orders[None, :] == panel_modes[0][:, None]).astype(jnp.bfloat16)
    picked = jnp.take(coefficients, panel_modes[1], axis=1)
    values = jnp.einsum("ms,smc->mc", owned, picked, preferred_element_type=jnp.float32)
    values = lax.ppermute(values.astype(jnp.bfloat16), "field", [(0, 1), (1, 0)])
    columns = doubled(values, "lat").astype(jnp.float32).reshape(2 * mode_count, snap_count)
    centered = (columns - jnp.mean(columns, axis=1, keepdims=True)).astype(jnp.bfloat16)

    coef_rows = coefficients.reshape(slot_count * deg_count * 2, snap_count)
    panel_values = lax.dot_general(
        coef_rows, centered, (((1,), (1,)), ((), ())), preferred_element_type=jnp.float32
    )
    panel_values = panel_values * (1.0 / (snap_count - 1))
    return panel_values.astype(jnp.bfloat16).reshape(1, slot_count, 2 * deg_count, 2 * mode_count)


def solution(mesh):
    placed = (P("field", None, None, "lat", None), P("lat", None, None), P(), P())
    return jax.shard_map(
        local, mesh=mesh, in_specs=placed, out_specs=P("field", "lat", None, None), check_vma=False
    )
```

```python
import math

import jax
import jax.numpy as jnp
import numpy as np
from jax import lax
from jax.experimental import pallas as pl
from jax.experimental.pallas import tpu as pltpu
from jax.sharding import PartitionSpec as P


def dft_table(lon_count, order_count):
    products = np.arange(lon_count)[:, None] * np.arange(order_count)[None, :] % lon_count
    angles = products * (2.0 * math.pi / lon_count)
    return np.stack([np.cos(angles), -np.sin(angles)], axis=1).astype(jnp.bfloat16)


def summed_other_field(block):
    count = lax.axis_size("lat")
    both = ("lat", "field")
    near = [(2 * i + f, 2 * i + 1 - f) for i in range(count) for f in range(2)]
    far = [(2 * i + f, 2 * (i ^ 1) + 1 - f) for i in range(count) for f in range(2)]
    block = lax.ppermute(block, both, near) + lax.ppermute(block, both, far)
    reach = 2
    while reach < count:
        block = block + lax.ppermute(block, "lat", [(i, i ^ reach) for i in range(count)])
        reach *= 2
    return block


def coefficient_kernel(orders_ref, parts_ref, place_ref, basis_ref, out_ref):
    order = orders_ref[pl.program_id(0)]
    wide = 2 * parts_ref.shape[3]
    pairs, degrees = basis_ref.shape[1], basis_ref.shape[2]
    parts = parts_ref[:, 0].reshape(2, pairs, wide // 2)
    by_pair = [
        lax.dot_general(
            parts[k], place_ref[...], (((0,), (0,)), ((), ())), preferred_element_type=jnp.float32
        ).astype(jnp.bfloat16)
        for k in range(2)
    ]
    both = jnp.dot(
        jnp.concatenate(by_pair, axis=0), basis_ref[0], preferred_element_type=jnp.float32
    )
    degree = lax.broadcasted_iota(jnp.int32, (1, degrees), 1)
    odd = ((degree - order) & 1) == 1
    keep = (degree >= order) & (order >= 0)
    chosen = jnp.where(odd, both[wide // 2 :], both[: wide // 2])
    out_ref[0] = jnp.where(keep, chosen, 0.0).astype(jnp.bfloat16)


def panel_kernel(coef_ref, centered_ref, out_ref, rows_ref, *, scale):
    degrees = coef_ref.shape[2]
    values = lax.dot_general(
        coef_ref[0], centered_ref[...], (((0,), (0,)), ((), ())), preferred_element_type=jnp.float32
    )
    values = values * scale
    half = values.shape[1] // 2
    rows_ref[pl.ds(0, degrees, stride=2), :] = values[:, :half]
    rows_ref[pl.ds(1, degrees, stride=2), :] = values[:, half:]
    out_ref[0, 0] = rows_ref[...].astype(jnp.bfloat16)


def local(fields_grid, basis, order_table, panel_modes):
    grid_one = fields_grid[0]
    snap_count, _, pair_count, lon_count = grid_one.shape
    group_count, slot_count = order_table.shape
    pair_total, deg_count = basis.shape[1], basis.shape[2]
    mode_count = panel_modes.shape[1]
    order_count = lon_count // 2
    wide = 2 * snap_count
    orders = order_table.reshape(-1)
    mode_order, mode_degree = panel_modes[0], panel_modes[1]
    group_index = lax.axis_index("lat")
    my_orders = lax.dynamic_slice_in_dim(order_table, group_index, 1, 0)[0]

    owned = my_orders[:, None] == mode_order[None, :]
    degree = lax.broadcasted_iota(jnp.int32, (1, deg_count, 1), 1)
    pick = (owned[:, None, :] & (degree == mode_degree[None, None, :])).astype(jnp.bfloat16)
    columns = jnp.einsum("sjl,slc->sjc", basis, pick, preferred_element_type=jnp.float32)
    columns = jnp.sum(columns, axis=0).astype(jnp.bfloat16)
    columns = columns.reshape(group_count, 1, pair_count * mode_count)
    columns = lax.all_to_all(columns, "lat", split_axis=0, concat_axis=0, tiled=True)
    columns = jnp.sum(columns.astype(jnp.float32), axis=(0, 1)).reshape(pair_count, mode_count)

    table = jnp.asarray(dft_table(lon_count, order_count))
    fourier = jnp.einsum("thjn,nrm->hjrtm", grid_one, table, preferred_element_type=jnp.float32)
    fourier = fourier * (1.0 / math.sqrt(lon_count))
    parts = jnp.stack([fourier[0] + fourier[1], fourier[0] - fourier[1]]).astype(jnp.bfloat16)
    parts = parts.reshape(2 * pair_count * wide, order_count)
    wanted = jnp.concatenate([orders, mode_order])
    placed = (wanted[:, None] == lax.broadcasted_iota(jnp.int32, (1, order_count), 1)).astype(
        jnp.bfloat16
    )
    sent = lax.dot_general(
        placed, parts, (((1,), (1,)), ((), ())), preferred_element_type=jnp.float32
    ).astype(jnp.bfloat16)
    mode_parts = sent[group_count * slot_count :].reshape(mode_count, 2, pair_count, wide)
    sent = sent[: group_count * slot_count]
    sent = sent.reshape(group_count, slot_count, 2 * pair_count, wide).transpose(0, 2, 1, 3)
    sent = sent.reshape(group_count, 2 * pair_count * slot_count, wide)
    received = lax.all_to_all(sent, "lat", split_axis=0, concat_axis=0, tiled=True)

    mode_odd = ((mode_degree - mode_order) % 2 == 1)[:, None, None]
    mode_side = jnp.where(mode_odd, mode_parts[:, 1], mode_parts[:, 0]).astype(jnp.float32)
    share = jnp.sum(mode_side * columns.T[:, :, None], axis=1)
    values = summed_other_field(share).astype(jnp.bfloat16).astype(jnp.float32)
    values = values.reshape(2 * mode_count, snap_count)
    centered = (values - jnp.mean(values, axis=1, keepdims=True)).astype(jnp.bfloat16).T
    blank = jnp.zeros_like(centered)
    centered = jnp.concatenate(
        [jnp.concatenate([centered, blank], 1), jnp.concatenate([blank, centered], 1)], 0
    )

    parts_in = received.transpose(1, 0, 2).reshape(2 * pair_count, slot_count, group_count, wide)
    source = lax.broadcasted_iota(jnp.int32, (pair_total, 1), 0)
    place = (
        pair_count * (source % group_count) + source // group_count
        == lax.broadcasted_iota(jnp.int32, (1, pair_total), 1)
    ).astype(jnp.bfloat16)
    coefficients = pl.pallas_call(
        coefficient_kernel,
        grid_spec=pltpu.PrefetchScalarGridSpec(
            num_scalar_prefetch=1,
            grid=(slot_count,),
            in_specs=[
                pl.BlockSpec((2 * pair_count, 1, group_count, wide), lambda s, o: (0, s, 0, 0)),
                pl.BlockSpec((pair_total, pair_total), lambda s, o: (0, 0)),
                pl.BlockSpec((1, pair_total, deg_count), lambda s, o: (s, 0, 0)),
            ],
            out_specs=pl.BlockSpec((1, wide, deg_count), lambda s, o: (s, 0, 0)),
        ),
        out_shape=jax.ShapeDtypeStruct((slot_count, wide, deg_count), jnp.bfloat16),
        name="coefficients",
    )(my_orders, parts_in, place, basis)
    return pl.pallas_call(
        lambda *refs: panel_kernel(*refs, scale=1.0 / (snap_count - 1)),
        grid=(slot_count,),
        in_specs=[
            pl.BlockSpec((1, wide, deg_count), lambda s: (s, 0, 0)),
            pl.BlockSpec((wide, 4 * mode_count), lambda s: (0, 0)),
        ],
        out_specs=pl.BlockSpec((1, 1, 2 * deg_count, 2 * mode_count), lambda s: (0, s, 0, 0)),
        scratch_shapes=[pltpu.VMEM((2 * deg_count, 2 * mode_count), jnp.float32)],
        out_shape=jax.ShapeDtypeStruct((1, slot_count, 2 * deg_count, 2 * mode_count), jnp.bfloat16),
        name="panel",
    )(coefficients, centered)


def solution(mesh):
    placed = (P("field", None, None, "lat", None), P("lat", None, None), P(), P())
    return jax.shard_map(
        local, mesh=mesh, in_specs=placed, out_specs=P("field", "lat", None, None), check_vma=False
    )
```

```python
import functools
import math

import jax
import jax.numpy as jnp
import numpy as np
from jax import lax
from jax.experimental import pallas as pl
from jax.experimental.pallas import tpu as pltpu
from jax.sharding import PartitionSpec as P


def dft_table(lon_count, order_count):
    products = np.arange(lon_count // 2)[:, None] * np.arange(order_count)[None, :] % lon_count
    angles = products * (2.0 * math.pi / lon_count)
    return np.stack([np.cos(angles), -np.sin(angles)], axis=1).astype(jnp.bfloat16)


def stepped(block, reach):
    count = lax.axis_size("lat")
    return block + lax.ppermute(block, "lat", [(i, i ^ reach) for i in range(count)])


def swapped_pair_sum(block):
    count = lax.axis_size("lat")
    both = ("lat", "field")
    near = [(2 * i + f, 2 * i + 1 - f) for i in range(count) for f in range(2)]
    far = [(2 * i + f, 2 * (i ^ 1) + 1 - f) for i in range(count) for f in range(2)]
    return lax.ppermute(block, both, near) + lax.ppermute(block, both, far)


def column_kernel(orders_ref, modes_ref, basis_ref, out_ref, held_ref, total_ref, sems):
    group = lax.axis_index("lat")
    slots, pairs, degrees = held_ref.shape
    modes = modes_ref.shape[1]
    owned = [modes_ref[0:1, :] == orders_ref[s, group] for s in range(slots)]
    wanted = [jnp.max(row.astype(jnp.int32)) > 0 for row in owned]
    copies = [
        pltpu.make_async_copy(basis_ref.at[s], held_ref.at[s], sems.at[s]) for s in range(slots)
    ]
    for s in range(slots):
        pl.when(wanted[s])(copies[s].start)
    total_ref[...] = jnp.zeros_like(total_ref)
    here = lax.broadcasted_iota(jnp.int32, (degrees, modes), 0) == modes_ref[1:2, :]
    for s in range(slots):

        @pl.when(wanted[s])
        def _():
            pick = (here & owned[s]).astype(jnp.float32).astype(jnp.bfloat16)
            copies[s].wait()
            total_ref[...] += jnp.dot(held_ref[s], pick, preferred_element_type=jnp.float32)

    share = pairs // out_ref.shape[0]
    for j in range(share):
        rows = total_ref[pl.ds(j, out_ref.shape[0], stride=share), :]
        out_ref[:, j * modes : (j + 1) * modes] = rows.astype(jnp.bfloat16)


def coefficient_kernel(
    orders_ref, received_ref, basis_ref, out_ref, held_ref, place_ref, sems, *, first
):
    group = lax.axis_index("lat")
    here, pairs, degrees = held_ref.shape
    slots = orders_ref.shape[0]
    sources, _, wide = received_ref.shape
    share = pairs // sources
    copies = [
        pltpu.make_async_copy(basis_ref.at[first + s], held_ref.at[s], sems.at[s])
        for s in range(here)
    ]
    for copy in copies:
        copy.start()
    row = lax.broadcasted_iota(jnp.int32, (pairs, pairs), 0)
    column = lax.broadcasted_iota(jnp.int32, (pairs, pairs), 1)
    place_ref[...] = (
        (share * (row % sources) + row // sources == column).astype(jnp.float32).astype(jnp.bfloat16)
    )
    degree = lax.broadcasted_iota(jnp.int32, (1, degrees), 1)
    for s in range(here):
        by_pair = []
        for parity in range(2):
            part = jnp.concatenate(
                [
                    received_ref[:, (parity * share + j) * slots + first + s, :]
                    for j in range(share)
                ],
                axis=0,
            )
            ordered = lax.dot_general(
                part, place_ref[...], (((0,), (0,)), ((), ())), preferred_element_type=jnp.float32
            )
            by_pair.append(ordered.astype(jnp.bfloat16))
        copies[s].wait()
        both = jnp.dot(
            jnp.concatenate(by_pair, axis=0), held_ref[s], preferred_element_type=jnp.float32
        )
        order = orders_ref[first + s, group]
        odd = ((degree - order) & 1) == 1
        keep = (degree >= order) & (order >= 0)
        chosen = jnp.where(odd, both[wide:], both[:wide])
        out_ref[s] = jnp.where(keep, chosen, 0.0).astype(jnp.bfloat16)


def panel_kernel(first_ref, last_ref, centered_ref, out_ref, rows_ref, sems, *, scale):
    half = first_ref.shape[0]
    copies = []
    for s in range(2 * half):
        block = first_ref[s] if s < half else last_ref[s - half]
        values = lax.dot_general(
            block, centered_ref[...], (((0,), (0,)), ((), ())), preferred_element_type=jnp.float32
        )
        rows_ref[s] = (values * scale).astype(jnp.bfloat16).reshape(rows_ref.shape[1:])
        copies.append(pltpu.make_async_copy(rows_ref.at[s], out_ref.at[0, s], sems.at[s]))
        copies[-1].start()
    for copy in copies:
        copy.wait()


def local(fields_grid, basis, order_table, panel_modes):
    grid_one = fields_grid[0]
    snap_count, _, pair_count, lon_count = grid_one.shape
    group_count, slot_count = order_table.shape
    pair_total, deg_count = basis.shape[1], basis.shape[2]
    mode_count = panel_modes.shape[1]
    order_count = lon_count // 2
    wide = 2 * snap_count
    in_vmem = pl.BlockSpec(memory_space=pltpu.VMEM)
    in_smem = pl.BlockSpec(memory_space=pltpu.SMEM)
    anywhere = pl.BlockSpec(memory_space=pl.ANY)
    mode_order, mode_degree = panel_modes[0], panel_modes[1]
    orders_by_slot = order_table.T

    columns = pl.pallas_call(
        column_kernel,
        in_specs=[in_smem, in_vmem, anywhere],
        out_specs=in_vmem,
        out_shape=jax.ShapeDtypeStruct((group_count, pair_count * mode_count), jnp.bfloat16),
        scratch_shapes=[
            pltpu.VMEM((slot_count, pair_total, deg_count), jnp.bfloat16),
            pltpu.VMEM((pair_total, mode_count), jnp.float32),
            pltpu.SemaphoreType.DMA((slot_count,)),
        ],
        name="columns",
    )(orders_by_slot, panel_modes, basis)
    columns = columns.reshape(group_count, 1, pair_count * mode_count)
    columns = lax.all_to_all(columns, "lat", split_axis=0, concat_axis=0, tiled=True)
    columns = jnp.sum(columns.astype(jnp.float32), axis=(0, 1)).reshape(pair_count, mode_count)

    table = jnp.asarray(dft_table(lon_count, order_count))
    halves = [
        jnp.einsum("thjn,nrm->hjrtm", half, table, preferred_element_type=jnp.float32)
        for half in (grid_one[..., :order_count], grid_one[..., order_count:])
    ]
    sign = 1.0 - 2.0 * (lax.iota(jnp.int32, order_count) % 2).astype(jnp.float32)
    fourier = (halves[0] + halves[1] * sign) * (1.0 / math.sqrt(lon_count))
    parts = jnp.stack([fourier[0] + fourier[1], fourier[0] - fourier[1]]).astype(jnp.bfloat16)
    parts = parts.reshape(2 * pair_count * wide, order_count)

    def rows_of(wanted):
        placed = wanted[:, None] == lax.broadcasted_iota(jnp.int32, (1, order_count), 1)
        rows = lax.dot_general(
            placed.astype(jnp.bfloat16),
            parts,
            (((1,), (1,)), ((), ())),
            preferred_element_type=jnp.float32,
        )
        return rows.astype(jnp.bfloat16)

    sent = rows_of(order_table.reshape(-1))
    sent = sent.reshape(group_count, slot_count, 2 * pair_count, wide).transpose(0, 2, 1, 3)
    sent = sent.reshape(group_count, 2 * pair_count * slot_count, wide)
    received = lax.all_to_all(sent, "lat", split_axis=0, concat_axis=0, tiled=True)

    mode_parts = rows_of(mode_order).reshape(mode_count, 2, pair_count, wide)
    mode_odd = ((mode_degree - mode_order) % 2 == 1)[:, None, None]
    mode_side = jnp.where(mode_odd, mode_parts[:, 1], mode_parts[:, 0]).astype(jnp.float32)
    values = swapped_pair_sum(jnp.sum(mode_side * columns.T[:, :, None], axis=1))
    reach = 2
    while 4 * reach < group_count:
        values = stepped(values, reach)
        reach *= 2

    def coefficients(block, first):
        count = slot_count // 2
        return pl.pallas_call(
            functools.partial(coefficient_kernel, first=first),
            in_specs=[in_smem, in_vmem, anywhere],
            out_specs=in_vmem,
            out_shape=jax.ShapeDtypeStruct((count, wide, deg_count), jnp.bfloat16),
            scratch_shapes=[
                pltpu.VMEM((count, pair_total, deg_count), jnp.bfloat16),
                pltpu.VMEM((pair_total, pair_total), jnp.bfloat16),
                pltpu.SemaphoreType.DMA((count,)),
            ],
            name="coefficients",
        )(orders_by_slot, block, basis)

    values, received = lax.optimization_barrier((values, received))
    first_half = coefficients(received, 0)
    values = stepped(values, reach)
    values, first_half, received = lax.optimization_barrier((values, first_half, received))
    last_half = coefficients(received, slot_count // 2)
    values = stepped(values, 2 * reach)
    values, last_half = lax.optimization_barrier((values, last_half))

    values = lax.reduce_precision(values, 8, 7).reshape(2 * mode_count, snap_count)
    centered = (values - jnp.mean(values, axis=1, keepdims=True)).astype(jnp.bfloat16).T
    blank = jnp.zeros_like(centered)
    centered = jnp.concatenate(
        [jnp.concatenate([centered, blank], 1), jnp.concatenate([blank, centered], 1)], 0
    )
    return pl.pallas_call(
        functools.partial(panel_kernel, scale=1.0 / (snap_count - 1)),
        in_specs=[in_vmem, in_vmem, in_vmem],
        out_specs=anywhere,
        out_shape=jax.ShapeDtypeStruct((1, slot_count, 2 * deg_count, 2 * mode_count), jnp.bfloat16),
        scratch_shapes=[
            pltpu.VMEM((slot_count, 2 * deg_count, 2 * mode_count), jnp.bfloat16),
            pltpu.SemaphoreType.DMA((slot_count,)),
        ],
        name="panel",
    )(first_half, last_half, centered)


def solution(mesh):
    placed = (P("field", None, None, "lat", None), P("lat", None, None), P(), P())
    return jax.shard_map(
        local, mesh=mesh, in_specs=placed, out_specs=P("field", "lat", None, None), check_vma=False
    )
```

```python
import functools
import math

import jax
import jax.numpy as jnp
import numpy as np
from jax import lax
from jax.experimental import pallas as pl
from jax.experimental.pallas import tpu as pltpu
from jax.sharding import PartitionSpec as P


def dft_table(lon_count, order_count):
    products = np.arange(lon_count // 2)[:, None] * np.arange(order_count)[None, :] % lon_count
    angles = products * (2.0 * math.pi / lon_count)
    return np.stack([np.cos(angles), -np.sin(angles)], axis=1).astype(jnp.bfloat16)


def from_far(block, reach):
    count = lax.axis_size("lat")
    return lax.ppermute(block, "lat", [(i, i ^ reach) for i in range(count)])


def stepped(block, reach):
    return block + from_far(block, reach)


def swapped_pair_sum(block):
    count = lax.axis_size("lat")
    both = ("lat", "field")
    near = [(2 * i + f, 2 * i + 1 - f) for i in range(count) for f in range(2)]
    far = [(2 * i + f, 2 * (i ^ 1) + 1 - f) for i in range(count) for f in range(2)]
    return lax.ppermute(block, both, near) + lax.ppermute(block, both, far)


def one_hot(condition):
    return condition.astype(jnp.float32).astype(jnp.bfloat16)


def column_kernel(orders_ref, modes_ref, basis_ref, out_ref, held_ref, total_ref, rows_ref, sems):
    group = lax.axis_index("lat")
    slots, pairs, degrees = held_ref.shape
    modes = modes_ref.shape[1]
    owned = [modes_ref[0:1, :] == orders_ref[s, group] for s in range(slots)]
    wanted = [jnp.max(row.astype(jnp.int32)) > 0 for row in owned]
    copies = [
        pltpu.make_async_copy(basis_ref.at[s], held_ref.at[s], sems.at[s]) for s in range(slots)
    ]
    for s in range(slots):
        pl.when(wanted[s])(copies[s].start)
    total_ref[...] = jnp.zeros_like(total_ref)
    here = lax.broadcasted_iota(jnp.int32, (degrees, modes), 0) == modes_ref[1:2, :]
    for s in range(slots):

        @pl.when(wanted[s])
        def _():
            pick = one_hot(here & owned[s])
            copies[s].wait()
            total_ref[...] += jnp.dot(held_ref[s], pick, preferred_element_type=jnp.float32)

    groups, halves, lanes = out_ref.shape
    share = pairs // groups
    blocks = [total_ref[pl.ds(j, groups, stride=share), :] for j in range(share)]
    blocks += [jnp.zeros_like(blocks[0])] * (halves * lanes // modes - share)
    per_half = lanes // modes
    for h in range(halves):
        half = jnp.concatenate(blocks[h * per_half : (h + 1) * per_half], axis=1)
        rows_ref[pl.ds(h, groups, stride=halves), :] = half
    out_ref[...] = rows_ref[...].astype(jnp.bfloat16).reshape(out_ref.shape)


def basis_kernel(
    values_ref, basis_ref, out_ref, same_ref, held_ref, rows_ref, sems, out_sems, *, sources
):
    same_ref[...] = values_ref[...]
    slots, pairs, _ = out_ref.shape
    share = pairs // sources
    copies = [
        pltpu.make_async_copy(basis_ref.at[s], held_ref.at[s], sems.at[s]) for s in range(slots)
    ]
    out_copies = [
        pltpu.make_async_copy(rows_ref.at[s], out_ref.at[s], out_sems.at[s]) for s in range(slots)
    ]
    for copy in copies:
        copy.start()
    row = lax.broadcasted_iota(jnp.int32, (pairs, pairs), 0)
    column = lax.broadcasted_iota(jnp.int32, (pairs, pairs), 1)
    place = one_hot(share * (row % sources) + row // sources == column)
    for s in range(slots):
        copies[s].wait()
        rows = jnp.dot(place, held_ref[s], preferred_element_type=jnp.float32)
        rows_ref[s] = rows.astype(jnp.bfloat16)
        out_copies[s].start()
    for copy in out_copies:
        copy.wait()


def coefficient_kernel(orders_ref, received_ref, basis_ref, out_ref, held_ref, sems, *, first):
    group = lax.axis_index("lat")
    slots, pairs, degrees = basis_ref.shape
    sources, _, wide = received_ref.shape
    share = pairs // sources
    here = out_ref.shape[0]
    copies = [
        pltpu.make_async_copy(basis_ref.at[first + s], held_ref.at[s], sems.at[s])
        for s in range(here)
    ]
    for copy in copies:
        copy.start()
    degree = lax.broadcasted_iota(jnp.int32, (1, degrees), 1)
    for s in range(here):
        sides = [
            jnp.concatenate(
                [
                    received_ref[:, (parity * share + j) * slots + first + s, :]
                    for j in range(share)
                ],
                axis=0,
            )
            for parity in range(2)
        ]
        copies[s].wait()
        both = lax.dot_general(
            jnp.concatenate(sides, axis=1),
            held_ref[s],
            (((0,), (0,)), ((), ())),
            preferred_element_type=jnp.float32,
        )
        order = orders_ref[first + s, group]
        odd = ((degree - order) & 1) == 1
        keep = (degree >= order) & (order >= 0)
        chosen = jnp.where(odd, both[wide:], both[:wide])
        out_ref[s] = jnp.where(keep, chosen, 0.0).astype(jnp.bfloat16)


def panel_kernel(first_ref, last_ref, values_ref, out_ref, rows_ref, sems, *, scale):
    modes, wide = values_ref.shape
    snaps = wide // 2
    values = values_ref[...].astype(jnp.bfloat16).astype(jnp.float32)
    mode = lax.broadcasted_iota(jnp.int32, (modes, 2 * modes), 0)
    column = lax.broadcasted_iota(jnp.int32, (modes, 2 * modes), 1)
    block = jnp.zeros((snaps, 2 * modes), jnp.float32)
    for u in range(2):
        part = values[:, u * snaps : (u + 1) * snaps]
        part = (part - jnp.mean(part, axis=1, keepdims=True)).astype(jnp.bfloat16)
        block += lax.dot_general(
            part,
            one_hot(2 * mode + u == column),
            (((0,), (0,)), ((), ())),
            preferred_element_type=jnp.float32,
        )
    block = block.astype(jnp.bfloat16)
    blank = jnp.zeros_like(block)
    centered = jnp.concatenate(
        [jnp.concatenate([block, blank], axis=1), jnp.concatenate([blank, block], axis=1)], axis=0
    )
    half = first_ref.shape[0]
    copies = []
    for s in range(2 * half):
        rows = first_ref[s] if s < half else last_ref[s - half]
        products = lax.dot_general(
            rows, centered, (((0,), (0,)), ((), ())), preferred_element_type=jnp.float32
        )
        rows_ref[s] = (products * scale).astype(jnp.bfloat16).reshape(rows_ref.shape[1:])
        copies.append(pltpu.make_async_copy(rows_ref.at[s], out_ref.at[0, s], sems.at[s]))
        copies[-1].start()
    for copy in copies:
        copy.wait()


def local(fields_grid, basis, order_table, panel_modes):
    grid_one = fields_grid[0]
    snap_count, _, pair_count, lon_count = grid_one.shape
    group_count, slot_count = order_table.shape
    pair_total, deg_count = basis.shape[1], basis.shape[2]
    mode_count = panel_modes.shape[1]
    order_count = lon_count // 2
    wide = 2 * snap_count
    in_vmem = pl.BlockSpec(memory_space=pltpu.VMEM)
    in_smem = pl.BlockSpec(memory_space=pltpu.SMEM)
    anywhere = pl.BlockSpec(memory_space=pl.ANY)
    mode_order, mode_degree = panel_modes[0], panel_modes[1]
    orders_by_slot = order_table.T
    in_hbm = pl.BlockSpec(memory_space=pltpu.HBM)
    roomy = pltpu.CompilerParams(vmem_limit_bytes=24 << 20)

    columns = pl.pallas_call(
        column_kernel,
        in_specs=[in_smem, in_vmem, in_hbm],
        out_specs=in_vmem,
        out_shape=jax.ShapeDtypeStruct((group_count, 2, wide), jnp.bfloat16),
        scratch_shapes=[
            pltpu.VMEM((slot_count, pair_total, deg_count), jnp.bfloat16),
            pltpu.VMEM((pair_total, mode_count), jnp.float32),
            pltpu.VMEM((2 * group_count, wide), jnp.float32),
            pltpu.SemaphoreType.DMA((slot_count,)),
        ],
        name="columns",
    )(orders_by_slot, panel_modes, pltpu.with_memory_space_constraint(basis, pltpu.HBM))
    columns = lax.all_to_all(columns, "lat", split_axis=0, concat_axis=0, tiled=True)
    columns = jnp.sum(columns.astype(jnp.float32), axis=0).reshape(-1, mode_count)[:pair_count]

    table = jnp.asarray(dft_table(lon_count, order_count))
    halves = [
        jnp.einsum("thjn,nrm->hjrtm", half, table, preferred_element_type=jnp.float32)
        for half in (grid_one[..., :order_count], grid_one[..., order_count:])
    ]
    sign = 1.0 - 2.0 * (lax.iota(jnp.int32, order_count) % 2).astype(jnp.float32)
    fourier = (halves[0] + halves[1] * sign) * (1.0 / math.sqrt(lon_count))
    parts = jnp.stack([fourier[0] + fourier[1], fourier[0] - fourier[1]]).astype(jnp.bfloat16)
    parts = parts.reshape(2 * pair_count * wide, order_count)

    def rows_of(wanted):
        placed = wanted[:, None] == lax.broadcasted_iota(jnp.int32, (1, order_count), 1)
        rows = lax.dot_general(
            placed.astype(jnp.bfloat16),
            parts,
            (((1,), (1,)), ((), ())),
            preferred_element_type=jnp.float32,
        )
        return rows.astype(jnp.bfloat16)

    sent = rows_of(order_table.reshape(-1))
    sent = sent.reshape(group_count, slot_count, 2 * pair_count, wide).transpose(0, 2, 1, 3)
    sent = sent.reshape(group_count, 2 * pair_count * slot_count, wide)
    received = lax.all_to_all(sent, "lat", split_axis=0, concat_axis=0, tiled=True)

    mode_parts = rows_of(mode_order).reshape(mode_count, 2, pair_count, wide)
    mode_odd = ((mode_degree - mode_order) % 2 == 1)[:, None, None]
    mode_side = jnp.where(mode_odd, mode_parts[:, 1], mode_parts[:, 0]).astype(jnp.float32)
    values = swapped_pair_sum(jnp.sum(mode_side * columns.T[:, :, None], axis=1))
    reach = 2
    while 8 * reach < group_count:
        values = stepped(values, reach)
        reach *= 2
    by_source, same = pl.pallas_call(
        functools.partial(basis_kernel, sources=group_count),
        in_specs=[in_vmem, in_hbm],
        out_specs=(in_hbm, in_vmem),
        out_shape=(
            pltpu.HBM(basis.shape, jnp.bfloat16),
            jax.ShapeDtypeStruct(values.shape, jnp.float32),
        ),
        scratch_shapes=[
            pltpu.VMEM(basis.shape, jnp.bfloat16),
            pltpu.VMEM(basis.shape, jnp.bfloat16),
            pltpu.SemaphoreType.DMA((slot_count,)),
            pltpu.SemaphoreType.DMA((slot_count,)),
        ],
        compiler_params=roomy,
        name="basis",
    )(values, pltpu.with_memory_space_constraint(basis, pltpu.HBM))
    values = same + from_far(values, reach)
    reach *= 2

    def coefficients(block, first):
        count = slot_count // 2
        return pl.pallas_call(
            functools.partial(coefficient_kernel, first=first),
            in_specs=[in_smem, in_vmem, in_hbm],
            out_specs=in_vmem,
            out_shape=pltpu.VMEM((count, wide, deg_count), jnp.bfloat16),
            scratch_shapes=[
                pltpu.VMEM((count, pair_total, deg_count), jnp.bfloat16),
                pltpu.SemaphoreType.DMA((count,)),
            ],
            compiler_params=roomy,
        name="coefficients",
        )(
            orders_by_slot,
            pltpu.with_memory_space_constraint(block, pltpu.VMEM),
            pltpu.with_memory_space_constraint(by_source, pltpu.HBM),
        )

    values, received = lax.optimization_barrier((values, received))
    first_half = coefficients(received, 0)
    values = stepped(values, reach)
    values, first_half, received = lax.optimization_barrier((values, first_half, received))
    last_half = coefficients(received, slot_count // 2)
    values = stepped(values, 2 * reach)
    return pl.pallas_call(
        functools.partial(panel_kernel, scale=1.0 / (snap_count - 1)),
        in_specs=[in_vmem, in_vmem, in_vmem],
        out_specs=anywhere,
        out_shape=jax.ShapeDtypeStruct((1, slot_count, 2 * deg_count, 2 * mode_count), jnp.bfloat16),
        scratch_shapes=[
            pltpu.VMEM((slot_count, 2 * deg_count, 2 * mode_count), jnp.bfloat16),
            pltpu.SemaphoreType.DMA((slot_count,)),
        ],
        compiler_params=roomy,
        name="panel",
    )(
        pltpu.with_memory_space_constraint(first_half, pltpu.VMEM),
        pltpu.with_memory_space_constraint(last_half, pltpu.VMEM),
        pltpu.with_memory_space_constraint(values, pltpu.VMEM),
    )


def solution(mesh):
    placed = (P("field", None, None, "lat", None), P("lat", None, None), P(), P())
    return jax.shard_map(
        local, mesh=mesh, in_specs=placed, out_specs=P("field", "lat", None, None), check_vma=False
    )
```

```python
import functools
import math

import jax
import jax.numpy as jnp
import numpy as np
from jax import lax
from jax.experimental import pallas as pl
from jax.experimental.pallas import tpu as pltpu
from jax.sharding import PartitionSpec as P


def dft_table(lon_count, order_count):
    products = np.arange(lon_count // 2)[:, None] * np.arange(order_count)[None, :] % lon_count
    angles = products * (2.0 * math.pi / lon_count)
    return np.stack([np.cos(angles), -np.sin(angles)], axis=1).astype(jnp.bfloat16)


def from_far(block, reach):
    count = lax.axis_size("lat")
    return lax.ppermute(block, "lat", [(i, i ^ reach) for i in range(count)])


def stepped(block, reach):
    return block + from_far(block, reach)


def swapped_pair_sum(block):
    count = lax.axis_size("lat")
    both = ("lat", "field")
    near = [(2 * i + f, 2 * i + 1 - f) for i in range(count) for f in range(2)]
    far = [(2 * i + f, 2 * (i ^ 1) + 1 - f) for i in range(count) for f in range(2)]
    return lax.ppermute(block, both, near) + lax.ppermute(block, both, far)


def one_hot(condition):
    return condition.astype(jnp.float32).astype(jnp.bfloat16)


def column_kernel(orders_ref, modes_ref, basis_ref, out_ref, held_ref, total_ref, rows_ref, sems):
    group = lax.axis_index("lat")
    slots, pairs, degrees = held_ref.shape
    modes = modes_ref.shape[1]
    owned = [modes_ref[0:1, :] == orders_ref[s, group] for s in range(slots)]
    wanted = [jnp.max(row.astype(jnp.int32)) > 0 for row in owned]
    copies = [
        pltpu.make_async_copy(basis_ref.at[s], held_ref.at[s], sems.at[s]) for s in range(slots)
    ]
    for s in range(slots):
        pl.when(wanted[s])(copies[s].start)
    total_ref[...] = jnp.zeros_like(total_ref)
    here = lax.broadcasted_iota(jnp.int32, (degrees, modes), 0) == modes_ref[1:2, :]
    for s in range(slots):

        @pl.when(wanted[s])
        def _():
            pick = one_hot(here & owned[s])
            copies[s].wait()
            total_ref[...] += jnp.dot(held_ref[s], pick, preferred_element_type=jnp.float32)

    groups, halves, lanes = out_ref.shape
    share = pairs // groups
    blocks = [total_ref[pl.ds(j, groups, stride=share), :] for j in range(share)]
    blocks += [jnp.zeros_like(blocks[0])] * (halves * lanes // modes - share)
    per_half = lanes // modes
    for h in range(halves):
        half = jnp.concatenate(blocks[h * per_half : (h + 1) * per_half], axis=1)
        rows_ref[pl.ds(h, groups, stride=halves), :] = half
    out_ref[...] = rows_ref[...].astype(jnp.bfloat16).reshape(out_ref.shape)


def basis_kernel(
    values_ref, basis_ref, out_ref, same_ref, held_ref, rows_ref, sems, out_sems, *, first, sources
):
    same_ref[...] = values_ref[...]
    slots, _, pairs = out_ref.shape
    share = pairs // sources
    copies = [
        pltpu.make_async_copy(basis_ref.at[first + s], held_ref.at[s], sems.at[s])
        for s in range(slots)
    ]
    out_copies = [
        pltpu.make_async_copy(rows_ref.at[s], out_ref.at[s], out_sems.at[s]) for s in range(slots)
    ]
    for copy in copies:
        copy.start()
    row = lax.broadcasted_iota(jnp.int32, (pairs, pairs), 0)
    column = lax.broadcasted_iota(jnp.int32, (pairs, pairs), 1)
    place = one_hot(share * (column % sources) + column // sources == row)
    for s in range(slots):
        copies[s].wait()
        rows = lax.dot_general(
            held_ref[s], place, (((0,), (0,)), ((), ())), preferred_element_type=jnp.float32
        )
        rows_ref[s] = rows.astype(jnp.bfloat16)
        out_copies[s].start()
    for copy in out_copies:
        copy.wait()


def centered_columns(values):
    modes, wide = values.shape
    snaps = wide // 2
    values = values.astype(jnp.bfloat16).astype(jnp.float32)
    mode = lax.broadcasted_iota(jnp.int32, (modes, 2 * modes), 0)
    column = lax.broadcasted_iota(jnp.int32, (modes, 2 * modes), 1)
    block = jnp.zeros((snaps, 2 * modes), jnp.float32)
    for u in range(2):
        part = values[:, u * snaps : (u + 1) * snaps]
        part = (part - jnp.mean(part, axis=1, keepdims=True)).astype(jnp.bfloat16)
        block += lax.dot_general(
            part,
            one_hot(2 * mode + u == column),
            (((0,), (0,)), ((), ())),
            preferred_element_type=jnp.float32,
        )
    block = block.astype(jnp.bfloat16)
    blank = jnp.zeros_like(block)
    return jnp.concatenate(
        [jnp.concatenate([block, blank], axis=1), jnp.concatenate([blank, block], axis=1)], axis=0
    )


def panel_kernel(
    orders_ref,
    received_ref,
    first_ref,
    last_ref,
    values_ref,
    out_ref,
    held_ref,
    rows_ref,
    sems,
    out_sems,
    *,
    scale,
):
    group = lax.axis_index("lat")
    slots, degrees, pairs = held_ref.shape
    half = slots // 2
    sources, _, wide = received_ref.shape
    share = pairs // sources
    copies = []
    for s in range(slots):
        source = first_ref.at[s] if s < half else last_ref.at[s - half]
        copies.append(pltpu.make_async_copy(source, held_ref.at[s], sems.at[s]))
        copies[s].start()
    out_copies = [
        pltpu.make_async_copy(rows_ref.at[s], out_ref.at[0, s], out_sems.at[s])
        for s in range(slots)
    ]
    centered = centered_columns(values_ref[...])
    degree = lax.broadcasted_iota(jnp.int32, (degrees, 1), 0)
    for s in range(slots):
        sides = [
            jnp.concatenate(
                [received_ref[:, (parity * share + j) * slots + s, :] for j in range(share)], axis=0
            )
            for parity in range(2)
        ]
        copies[s].wait()
        both = jnp.dot(
            held_ref[s], jnp.concatenate(sides, axis=1), preferred_element_type=jnp.float32
        )
        order = orders_ref[s, group]
        odd = ((degree - order) & 1) == 1
        keep = (degree >= order) & (order >= 0)
        chosen = jnp.where(odd, both[:, wide:], both[:, :wide])
        coefficients = jnp.where(keep, chosen, 0.0).astype(jnp.bfloat16)
        products = jnp.dot(coefficients, centered, preferred_element_type=jnp.float32)
        rows_ref[s] = (products * scale).astype(jnp.bfloat16).reshape(rows_ref.shape[1:])
        out_copies[s].start()
    for copy in out_copies:
        copy.wait()


def local(fields_grid, basis, order_table, panel_modes):
    grid_one = fields_grid[0]
    snap_count, _, pair_count, lon_count = grid_one.shape
    group_count, slot_count = order_table.shape
    pair_total, deg_count = basis.shape[1], basis.shape[2]
    mode_count = panel_modes.shape[1]
    order_count = lon_count // 2
    wide = 2 * snap_count
    in_vmem = pl.BlockSpec(memory_space=pltpu.VMEM)
    in_smem = pl.BlockSpec(memory_space=pltpu.SMEM)
    anywhere = pl.BlockSpec(memory_space=pl.ANY)
    mode_order, mode_degree = panel_modes[0], panel_modes[1]
    orders_by_slot = order_table.T
    in_hbm = pl.BlockSpec(memory_space=pltpu.HBM)
    roomy = pltpu.CompilerParams(vmem_limit_bytes=24 << 20)

    columns = pl.pallas_call(
        column_kernel,
        in_specs=[in_smem, in_vmem, in_hbm],
        out_specs=in_vmem,
        out_shape=jax.ShapeDtypeStruct((group_count, 2, wide), jnp.bfloat16),
        scratch_shapes=[
            pltpu.VMEM((slot_count, pair_total, deg_count), jnp.bfloat16),
            pltpu.VMEM((pair_total, mode_count), jnp.float32),
            pltpu.VMEM((2 * group_count, wide), jnp.float32),
            pltpu.SemaphoreType.DMA((slot_count,)),
        ],
        name="columns",
    )(orders_by_slot, panel_modes, pltpu.with_memory_space_constraint(basis, pltpu.HBM))
    columns = lax.all_to_all(columns, "lat", split_axis=0, concat_axis=0, tiled=True)
    columns = jnp.sum(columns.astype(jnp.float32), axis=0).reshape(-1, mode_count)[:pair_count]

    table = jnp.asarray(dft_table(lon_count, order_count))
    products = [
        jnp.einsum("thjn,nrm->hjrtm", half, table, preferred_element_type=jnp.float32)
        for half in (grid_one[..., :order_count], grid_one[..., order_count:])
    ]
    sign = 1.0 - 2.0 * (lax.iota(jnp.int32, order_count) % 2).astype(jnp.float32)
    fourier = (products[0] + products[1] * sign) * (1.0 / math.sqrt(lon_count))
    parts = jnp.stack([fourier[0] + fourier[1], fourier[0] - fourier[1]]).astype(jnp.bfloat16)
    parts = parts.reshape(2 * pair_count * wide, order_count)

    def rows_of(wanted):
        placed = wanted[:, None] == lax.broadcasted_iota(jnp.int32, (1, order_count), 1)
        rows = lax.dot_general(
            placed.astype(jnp.bfloat16),
            parts,
            (((1,), (1,)), ((), ())),
            preferred_element_type=jnp.float32,
        )
        return rows.astype(jnp.bfloat16)

    sent = rows_of(order_table.reshape(-1))
    sent = sent.reshape(group_count, slot_count, 2 * pair_count, wide).transpose(0, 2, 1, 3)
    sent = sent.reshape(group_count, 2 * pair_count * slot_count, wide)
    received = lax.all_to_all(sent, "lat", split_axis=0, concat_axis=0, tiled=True)

    mode_parts = rows_of(mode_order).reshape(mode_count, 2, pair_count, wide)
    mode_odd = ((mode_degree - mode_order) % 2 == 1)[:, None, None]
    mode_side = jnp.where(mode_odd, mode_parts[:, 1], mode_parts[:, 0]).astype(jnp.float32)
    values = swapped_pair_sum(jnp.sum(mode_side * columns.T[:, :, None], axis=1))
    halves = []
    for reach in (2, 4, 8):
        if reach == 2:
            values = stepped(values, reach)
            continue
        count = slot_count // 2
        half, same = pl.pallas_call(
            functools.partial(basis_kernel, first=len(halves) * count, sources=group_count),
            in_specs=[in_vmem, in_hbm],
            out_specs=(in_hbm, in_vmem),
            out_shape=(
                pltpu.HBM((count, deg_count, pair_total), jnp.bfloat16),
                jax.ShapeDtypeStruct(values.shape, jnp.float32),
            ),
            scratch_shapes=[
                pltpu.VMEM((count, pair_total, deg_count), jnp.bfloat16),
                pltpu.VMEM((count, deg_count, pair_total), jnp.bfloat16),
                pltpu.SemaphoreType.DMA((count,)),
                pltpu.SemaphoreType.DMA((count,)),
            ],
            compiler_params=roomy,
            name="basis",
        )(values, pltpu.with_memory_space_constraint(basis, pltpu.HBM))
        halves.append(pltpu.with_memory_space_constraint(half, pltpu.HBM))
        values = same + from_far(values, reach)
    plane = 16
    own = values.astype(jnp.bfloat16)
    for step in range(1, group_count // plane):
        route = [(i, (i + step * plane) % group_count) for i in range(group_count)]
        values = values + lax.ppermute(own, "lat", route).astype(jnp.float32)
    return pl.pallas_call(
        functools.partial(panel_kernel, scale=1.0 / (snap_count - 1)),
        in_specs=[in_smem, in_vmem, in_hbm, in_hbm, in_vmem],
        out_specs=anywhere,
        out_shape=jax.ShapeDtypeStruct((1, slot_count, 2 * deg_count, 2 * mode_count), jnp.bfloat16),
        scratch_shapes=[
            pltpu.VMEM((slot_count, deg_count, pair_total), jnp.bfloat16),
            pltpu.VMEM((slot_count, 2 * deg_count, 2 * mode_count), jnp.bfloat16),
            pltpu.SemaphoreType.DMA((slot_count,)),
            pltpu.SemaphoreType.DMA((slot_count,)),
        ],
        compiler_params=roomy,
        name="panel",
    )(
        orders_by_slot,
        pltpu.with_memory_space_constraint(received, pltpu.VMEM),
        *halves,
        pltpu.with_memory_space_constraint(values, pltpu.VMEM),
    )


def solution(mesh):
    placed = (P("field", None, None, "lat", None), P("lat", None, None), P(), P())
    return jax.shard_map(
        local, mesh=mesh, in_specs=placed, out_specs=P("field", "lat", None, None), check_vma=False
    )
```

```python
import functools
import math

import jax
import jax.numpy as jnp
import numpy as np
from jax import lax
from jax.experimental import pallas as pl
from jax.experimental.pallas import tpu as pltpu
from jax.sharding import PartitionSpec as P


def dft_table(lon_count, order_count):
    products = np.arange(lon_count // 2)[:, None] * np.arange(order_count)[None, :] % lon_count
    angles = products * (2.0 * math.pi / lon_count)
    return np.stack([np.cos(angles), -np.sin(angles)], axis=1).astype(jnp.bfloat16)


def from_far(block, reach):
    count = lax.axis_size("lat")
    return lax.ppermute(block, "lat", [(i, i ^ reach) for i in range(count)])


def stepped(block, reach):
    return block + from_far(block, reach)


def swapped_pair_sum(block):
    count = lax.axis_size("lat")
    both = ("lat", "field")
    near = [(2 * i + f, 2 * i + 1 - f) for i in range(count) for f in range(2)]
    far = [(2 * i + f, 2 * (i ^ 1) + 1 - f) for i in range(count) for f in range(2)]
    return lax.ppermute(block, both, near) + lax.ppermute(block, both, far)


def one_hot(condition):
    return condition.astype(jnp.float32).astype(jnp.bfloat16)


def column_kernel(orders_ref, modes_ref, basis_ref, out_ref, held_ref, total_ref, rows_ref, sems):
    group = lax.axis_index("lat")
    slots, pairs, degrees = held_ref.shape
    modes = modes_ref.shape[1]
    owned = [modes_ref[0:1, :] == orders_ref[s, group] for s in range(slots)]
    wanted = [jnp.max(row.astype(jnp.int32)) > 0 for row in owned]
    copies = [
        pltpu.make_async_copy(basis_ref.at[s], held_ref.at[s], sems.at[s]) for s in range(slots)
    ]
    for s in range(slots):
        pl.when(wanted[s])(copies[s].start)
    total_ref[...] = jnp.zeros_like(total_ref)
    here = lax.broadcasted_iota(jnp.int32, (degrees, modes), 0) == modes_ref[1:2, :]
    for s in range(slots):

        @pl.when(wanted[s])
        def _():
            pick = one_hot(here & owned[s])
            copies[s].wait()
            total_ref[...] += jnp.dot(held_ref[s], pick, preferred_element_type=jnp.float32)

    groups, halves, lanes = out_ref.shape
    share = pairs // groups
    blocks = [total_ref[pl.ds(j, groups, stride=share), :] for j in range(share)]
    blocks += [jnp.zeros_like(blocks[0])] * (halves * lanes // modes - share)
    per_half = lanes // modes
    for h in range(halves):
        half = jnp.concatenate(blocks[h * per_half : (h + 1) * per_half], axis=1)
        rows_ref[pl.ds(h, groups, stride=halves), :] = half
    out_ref[...] = rows_ref[...].astype(jnp.bfloat16).reshape(out_ref.shape)


def basis_kernel(
    values_ref, basis_ref, out_ref, same_ref, held_ref, rows_ref, sems, out_sems, *, first, sources
):
    same_ref[...] = values_ref[...]
    slots, _, pairs = out_ref.shape
    share = pairs // sources
    copies = [
        pltpu.make_async_copy(basis_ref.at[first + s], held_ref.at[s], sems.at[s])
        for s in range(slots)
    ]
    out_copies = [
        pltpu.make_async_copy(rows_ref.at[s], out_ref.at[s], out_sems.at[s]) for s in range(slots)
    ]
    for copy in copies:
        copy.start()
    row = lax.broadcasted_iota(jnp.int32, (pairs, pairs), 0)
    column = lax.broadcasted_iota(jnp.int32, (pairs, pairs), 1)
    place = one_hot(share * (column % sources) + column // sources == row)
    for s in range(slots):
        copies[s].wait()
        rows = lax.dot_general(
            held_ref[s], place, (((0,), (0,)), ((), ())), preferred_element_type=jnp.float32
        )
        rows_ref[s] = rows.astype(jnp.bfloat16)
        out_copies[s].start()
    for copy in out_copies:
        copy.wait()


def centered_columns(values):
    modes, wide = values.shape
    snaps = wide // 2
    values = values.astype(jnp.bfloat16).astype(jnp.float32)
    mode = lax.broadcasted_iota(jnp.int32, (modes, 2 * modes), 0)
    column = lax.broadcasted_iota(jnp.int32, (modes, 2 * modes), 1)
    block = jnp.zeros((snaps, 2 * modes), jnp.float32)
    for u in range(2):
        part = values[:, u * snaps : (u + 1) * snaps]
        part = (part - jnp.mean(part, axis=1, keepdims=True)).astype(jnp.bfloat16)
        block += lax.dot_general(
            part,
            one_hot(2 * mode + u == column),
            (((0,), (0,)), ((), ())),
            preferred_element_type=jnp.float32,
        )
    block = block.astype(jnp.bfloat16)
    blank = jnp.zeros_like(block)
    return jnp.concatenate(
        [jnp.concatenate([block, blank], axis=1), jnp.concatenate([blank, block], axis=1)], axis=0
    )


def panel_kernel(
    orders_ref,
    received_ref,
    first_ref,
    last_ref,
    values_ref,
    out_ref,
    held_ref,
    rows_ref,
    sems,
    out_sems,
    *,
    scale,
):
    group = lax.axis_index("lat")
    slots, degrees, _ = held_ref.shape
    half = slots // 2
    wide = received_ref.shape[2]
    parts = received_ref.shape[0] // slots
    copies = []
    for s in range(slots):
        source = first_ref.at[s] if s < half else last_ref.at[s - half]
        copies.append(pltpu.make_async_copy(source, held_ref.at[s], sems.at[s]))
        copies[s].start()
    out_copies = [
        pltpu.make_async_copy(rows_ref.at[s], out_ref.at[0, s], out_sems.at[s])
        for s in range(slots)
    ]
    centered = centered_columns(values_ref[...])
    degree = lax.broadcasted_iota(jnp.int32, (degrees, 1), 0)

    def of_both_parities(s):
        rows = [received_ref[k * slots + s] for k in range(parts)]
        sides = [
            jnp.concatenate(rows[: parts // 2], axis=0),
            jnp.concatenate(rows[parts // 2 :], axis=0),
        ]
        return jnp.dot(
            held_ref[s], jnp.concatenate(sides, axis=1), preferred_element_type=jnp.float32
        )

    def finish(s, both):
        order = orders_ref[s, group]
        odd = ((degree - order) & 1) == 1
        keep = (degree >= order) & (order >= 0)
        chosen = jnp.where(odd, both[:, wide:], both[:, :wide])
        coefficients = jnp.where(keep, chosen, 0.0).astype(jnp.bfloat16)
        products = jnp.dot(coefficients, centered, preferred_element_type=jnp.float32)
        rows_ref[s] = (products * scale).astype(jnp.bfloat16).reshape(rows_ref.shape[1:])

    begun = []
    for start in range(0, slots + 2, 2):
        coming = range(start, min(start + 2, slots))
        for s in coming:
            copies[s].wait()
        new = [(s, of_both_parities(s)) for s in coming]
        for s, both in begun:
            finish(s, both)
        for s, _ in begun:
            out_copies[s].start()
        begun = new
    for copy in out_copies:
        copy.wait()


def local(fields_grid, basis, order_table, panel_modes):
    grid_one = fields_grid[0]
    snap_count, _, pair_count, lon_count = grid_one.shape
    group_count, slot_count = order_table.shape
    pair_total, deg_count = basis.shape[1], basis.shape[2]
    mode_count = panel_modes.shape[1]
    order_count = lon_count // 2
    wide = 2 * snap_count
    in_vmem = pl.BlockSpec(memory_space=pltpu.VMEM)
    in_smem = pl.BlockSpec(memory_space=pltpu.SMEM)
    anywhere = pl.BlockSpec(memory_space=pl.ANY)
    mode_order, mode_degree = panel_modes[0], panel_modes[1]
    orders_by_slot = order_table.T
    in_hbm = pl.BlockSpec(memory_space=pltpu.HBM)
    roomy = pltpu.CompilerParams(vmem_limit_bytes=32 << 20)

    columns = pl.pallas_call(
        column_kernel,
        in_specs=[in_smem, in_vmem, in_hbm],
        out_specs=in_vmem,
        out_shape=jax.ShapeDtypeStruct((group_count, 2, wide), jnp.bfloat16),
        scratch_shapes=[
            pltpu.VMEM((slot_count, pair_total, deg_count), jnp.bfloat16),
            pltpu.VMEM((pair_total, mode_count), jnp.float32),
            pltpu.VMEM((2 * group_count, wide), jnp.float32),
            pltpu.SemaphoreType.DMA((slot_count,)),
        ],
        name="columns",
    )(orders_by_slot, panel_modes, pltpu.with_memory_space_constraint(basis, pltpu.HBM))
    columns = lax.all_to_all(columns, "lat", split_axis=0, concat_axis=0, tiled=True)
    columns = jnp.sum(columns.astype(jnp.float32), axis=0).reshape(-1, mode_count)[:pair_count]

    table = jnp.asarray(dft_table(lon_count, order_count))
    products = [
        jnp.einsum("thjn,nrm->hjrtm", half, table, preferred_element_type=jnp.float32)
        for half in (grid_one[..., :order_count], grid_one[..., order_count:])
    ]
    sign = 1.0 - 2.0 * (lax.iota(jnp.int32, order_count) % 2).astype(jnp.float32)
    fourier = (products[0] + products[1] * sign) * (1.0 / math.sqrt(lon_count))
    parts = jnp.stack([fourier[0] + fourier[1], fourier[0] - fourier[1]]).astype(jnp.bfloat16)
    parts = parts.reshape(2 * pair_count * wide, order_count)

    def rows_of(wanted):
        placed = wanted[:, None] == lax.broadcasted_iota(jnp.int32, (1, order_count), 1)
        rows = lax.dot_general(
            placed.astype(jnp.bfloat16),
            parts,
            (((1,), (1,)), ((), ())),
            preferred_element_type=jnp.float32,
        )
        return rows.astype(jnp.bfloat16)

    sent = rows_of(order_table.reshape(-1))
    sent = sent.reshape(group_count, slot_count, 2 * pair_count, wide).transpose(0, 2, 1, 3)
    sent = sent.reshape(group_count, 2 * pair_count * slot_count, wide)
    received = lax.all_to_all(sent, "lat", split_axis=0, concat_axis=0, tiled=True)

    mode_parts = rows_of(mode_order).reshape(mode_count, 2, pair_count, wide)
    mode_odd = ((mode_degree - mode_order) % 2 == 1)[:, None, None]
    mode_side = jnp.where(mode_odd, mode_parts[:, 1], mode_parts[:, 0]).astype(jnp.float32)
    values = swapped_pair_sum(jnp.sum(mode_side * columns.T[:, :, None], axis=1))
    halves = []
    for reach in (2, 4, 8):
        if reach == 2:
            values = stepped(values, reach)
            continue
        count = slot_count // 2
        half, same = pl.pallas_call(
            functools.partial(basis_kernel, first=len(halves) * count, sources=group_count),
            in_specs=[in_vmem, in_hbm],
            out_specs=(in_hbm, in_vmem),
            out_shape=(
                pltpu.HBM((count, deg_count, pair_total), jnp.bfloat16),
                jax.ShapeDtypeStruct(values.shape, jnp.float32),
            ),
            scratch_shapes=[
                pltpu.VMEM((count, pair_total, deg_count), jnp.bfloat16),
                pltpu.VMEM((count, deg_count, pair_total), jnp.bfloat16),
                pltpu.SemaphoreType.DMA((count,)),
                pltpu.SemaphoreType.DMA((count,)),
            ],
            compiler_params=roomy,
            name="basis",
        )(values, pltpu.with_memory_space_constraint(basis, pltpu.HBM))
        halves.append(pltpu.with_memory_space_constraint(half, pltpu.HBM))
        values = same + from_far(values, reach)
    plane = 16
    own = values.astype(jnp.bfloat16)
    for step in range(1, group_count // plane):
        route = [(i, (i + step * plane) % group_count) for i in range(group_count)]
        values = values + lax.ppermute(own, "lat", route).astype(jnp.float32)
    return pl.pallas_call(
        functools.partial(panel_kernel, scale=1.0 / (snap_count - 1)),
        in_specs=[in_smem, in_vmem, in_hbm, in_hbm, in_vmem],
        out_specs=anywhere,
        out_shape=jax.ShapeDtypeStruct((1, slot_count, 2 * deg_count, 2 * mode_count), jnp.bfloat16),
        scratch_shapes=[
            pltpu.VMEM((slot_count, deg_count, pair_total), jnp.bfloat16),
            pltpu.VMEM((slot_count, 2 * deg_count, 2 * mode_count), jnp.bfloat16),
            pltpu.SemaphoreType.DMA((slot_count,)),
            pltpu.SemaphoreType.DMA((slot_count,)),
        ],
        compiler_params=roomy,
        name="panel",
    )(
        orders_by_slot,
        pltpu.with_memory_space_constraint(received.transpose(1, 0, 2), pltpu.VMEM),
        *halves,
        pltpu.with_memory_space_constraint(values, pltpu.VMEM),
    )


def solution(mesh):
    placed = (P("field", None, None, "lat", None), P("lat", None, None), P(), P())
    return jax.shard_map(
        local, mesh=mesh, in_specs=placed, out_specs=P("field", "lat", None, None), check_vma=False
    )
```

```python
import functools
import math

import jax
import jax.numpy as jnp
import numpy as np
from jax import lax
from jax.experimental import pallas as pl
from jax.experimental.pallas import tpu as pltpu
from jax.sharding import PartitionSpec as P


def dft_table(lon_count, order_count):
    products = np.arange(lon_count // 2)[:, None] * np.arange(order_count)[None, :] % lon_count
    angles = products * (2.0 * math.pi / lon_count)
    return np.stack([np.cos(angles), -np.sin(angles)], axis=1).astype(jnp.bfloat16)


def from_far(block, reach):
    count = lax.axis_size("lat")
    return lax.ppermute(block, "lat", [(i, i ^ reach) for i in range(count)])


def stepped(block, reach):
    return block + from_far(block, reach)


def swapped_pair_sum(block):
    count = lax.axis_size("lat")
    both = ("lat", "field")
    near = [(2 * i + f, 2 * i + 1 - f) for i in range(count) for f in range(2)]
    far = [(2 * i + f, 2 * (i ^ 1) + 1 - f) for i in range(count) for f in range(2)]
    return lax.ppermute(block, both, near) + lax.ppermute(block, both, far)


def one_hot(condition):
    return condition.astype(jnp.float32).astype(jnp.bfloat16)


def column_kernel(orders_ref, modes_ref, basis_ref, out_ref, held_ref, total_ref, rows_ref, sems):
    group = lax.axis_index("lat")
    slots, pairs, degrees = held_ref.shape
    modes = modes_ref.shape[1]
    owned = [modes_ref[0:1, :] == orders_ref[s, group] for s in range(slots)]
    wanted = [jnp.max(row.astype(jnp.int32)) > 0 for row in owned]
    copies = [
        pltpu.make_async_copy(basis_ref.at[s], held_ref.at[s], sems.at[s]) for s in range(slots)
    ]
    for s in range(slots):
        pl.when(wanted[s])(copies[s].start)
    total_ref[...] = jnp.zeros_like(total_ref)
    here = lax.broadcasted_iota(jnp.int32, (degrees, modes), 0) == modes_ref[1:2, :]
    for s in range(slots):

        @pl.when(wanted[s])
        def _():
            pick = one_hot(here & owned[s])
            copies[s].wait()
            total_ref[...] += jnp.dot(held_ref[s], pick, preferred_element_type=jnp.float32)

    groups, halves, lanes = out_ref.shape
    share = pairs // groups
    blocks = [total_ref[pl.ds(j, groups, stride=share), :] for j in range(share)]
    blocks += [jnp.zeros_like(blocks[0])] * (halves * lanes // modes - share)
    per_half = lanes // modes
    for h in range(halves):
        half = jnp.concatenate(blocks[h * per_half : (h + 1) * per_half], axis=1)
        rows_ref[pl.ds(h, groups, stride=halves), :] = half
    out_ref[...] = rows_ref[...].astype(jnp.bfloat16).reshape(out_ref.shape)


def basis_kernel(
    values_ref, basis_ref, out_ref, same_ref, held_ref, rows_ref, sems, out_sems, *, first, sources
):
    same_ref[...] = values_ref[...]
    slots, _, pairs = out_ref.shape
    share = pairs // sources
    copies = [
        pltpu.make_async_copy(basis_ref.at[first + s], held_ref.at[s], sems.at[s])
        for s in range(slots)
    ]
    out_copies = [
        pltpu.make_async_copy(rows_ref.at[s], out_ref.at[s], out_sems.at[s]) for s in range(slots)
    ]
    for copy in copies:
        copy.start()
    row = lax.broadcasted_iota(jnp.int32, (pairs, pairs), 0)
    column = lax.broadcasted_iota(jnp.int32, (pairs, pairs), 1)
    place = one_hot(share * (column % sources) + column // sources == row)
    for s in range(slots):
        copies[s].wait()
        rows = lax.dot_general(
            held_ref[s], place, (((0,), (0,)), ((), ())), preferred_element_type=jnp.float32
        )
        rows_ref[s] = rows.astype(jnp.bfloat16)
        out_copies[s].start()
    for copy in out_copies:
        copy.wait()


def centered_columns(values):
    modes, wide = values.shape
    snaps = wide // 2
    values = values.astype(jnp.bfloat16).astype(jnp.float32)
    mode = lax.broadcasted_iota(jnp.int32, (modes, 2 * modes), 0)
    column = lax.broadcasted_iota(jnp.int32, (modes, 2 * modes), 1)
    block = jnp.zeros((snaps, 2 * modes), jnp.float32)
    for u in range(2):
        part = values[:, u * snaps : (u + 1) * snaps]
        part = (part - jnp.mean(part, axis=1, keepdims=True)).astype(jnp.bfloat16)
        block += lax.dot_general(
            part,
            one_hot(2 * mode + u == column),
            (((0,), (0,)), ((), ())),
            preferred_element_type=jnp.float32,
        )
    block = block.astype(jnp.bfloat16)
    blank = jnp.zeros_like(block)
    return jnp.concatenate(
        [jnp.concatenate([block, blank], axis=1), jnp.concatenate([blank, block], axis=1)], axis=0
    )


def panel_kernel(
    orders_ref,
    received_ref,
    values_ref,
    *refs,
    scale,
):
    *basis_refs, out_ref, held_ref, rows_ref, sems, out_sems = refs
    group = lax.axis_index("lat")
    slots, degrees, _ = held_ref.shape
    wide = received_ref.shape[2]
    parts = received_ref.shape[0] // slots
    sources = [ref.at[i] for ref in basis_refs for i in range(ref.shape[0])]
    copies = []
    for s in range(slots):
        copies.append(pltpu.make_async_copy(sources[s], held_ref.at[s], sems.at[s]))
        copies[s].start()
    out_copies = [
        pltpu.make_async_copy(rows_ref.at[s], out_ref.at[0, s], out_sems.at[s])
        for s in range(slots)
    ]
    centered = centered_columns(values_ref[...])
    degree = lax.broadcasted_iota(jnp.int32, (degrees, 1), 0)

    def of_both_parities(s):
        rows = [received_ref[k * slots + s] for k in range(parts)]
        sides = [
            jnp.concatenate(rows[: parts // 2], axis=0),
            jnp.concatenate(rows[parts // 2 :], axis=0),
        ]
        return jnp.dot(
            held_ref[s], jnp.concatenate(sides, axis=1), preferred_element_type=jnp.float32
        )

    def finish(s, both):
        order = orders_ref[s, group]
        odd = ((degree - order) & 1) == 1
        keep = (degree >= order) & (order >= 0)
        chosen = jnp.where(odd, both[:, wide:], both[:, :wide])
        coefficients = jnp.where(keep, chosen, 0.0).astype(jnp.bfloat16)
        products = jnp.dot(coefficients, centered, preferred_element_type=jnp.float32)
        rows_ref[s] = (products * scale).astype(jnp.bfloat16).reshape(rows_ref.shape[1:])

    begun = []
    for start in range(0, slots + 2, 2):
        coming = range(start, min(start + 2, slots))
        for s in coming:
            copies[s].wait()
        new = [(s, of_both_parities(s)) for s in coming]
        for s, both in begun:
            finish(s, both)
        for s, _ in begun:
            out_copies[s].start()
        begun = new
    for copy in out_copies:
        copy.wait()


def local(fields_grid, basis, order_table, panel_modes):
    grid_one = fields_grid[0]
    snap_count, _, pair_count, lon_count = grid_one.shape
    group_count, slot_count = order_table.shape
    pair_total, deg_count = basis.shape[1], basis.shape[2]
    mode_count = panel_modes.shape[1]
    order_count = lon_count // 2
    wide = 2 * snap_count
    in_vmem = pl.BlockSpec(memory_space=pltpu.VMEM)
    in_smem = pl.BlockSpec(memory_space=pltpu.SMEM)
    anywhere = pl.BlockSpec(memory_space=pl.ANY)
    mode_order, mode_degree = panel_modes[0], panel_modes[1]
    orders_by_slot = order_table.T
    in_hbm = pl.BlockSpec(memory_space=pltpu.HBM)
    roomy = pltpu.CompilerParams(vmem_limit_bytes=32 << 20)

    columns = pl.pallas_call(
        column_kernel,
        in_specs=[in_smem, in_vmem, in_hbm],
        out_specs=in_vmem,
        out_shape=jax.ShapeDtypeStruct((group_count, 2, wide), jnp.bfloat16),
        scratch_shapes=[
            pltpu.VMEM((slot_count, pair_total, deg_count), jnp.bfloat16),
            pltpu.VMEM((pair_total, mode_count), jnp.float32),
            pltpu.VMEM((2 * group_count, wide), jnp.float32),
            pltpu.SemaphoreType.DMA((slot_count,)),
        ],
        name="columns",
    )(orders_by_slot, panel_modes, pltpu.with_memory_space_constraint(basis, pltpu.HBM))
    columns = lax.all_to_all(columns, "lat", split_axis=0, concat_axis=0, tiled=True)
    columns = jnp.sum(columns.astype(jnp.float32), axis=0).reshape(-1, mode_count)[:pair_count]

    table = jnp.asarray(dft_table(lon_count, order_count))
    products = [
        jnp.einsum("thjn,nrm->hjrtm", half, table, preferred_element_type=jnp.float32)
        for half in (grid_one[..., :order_count], grid_one[..., order_count:])
    ]
    sign = 1.0 - 2.0 * (lax.iota(jnp.int32, order_count) % 2).astype(jnp.float32)
    fourier = (products[0] + products[1] * sign) * (1.0 / math.sqrt(lon_count))
    parts = jnp.stack([fourier[0] + fourier[1], fourier[0] - fourier[1]]).astype(jnp.bfloat16)
    parts = parts.reshape(2 * pair_count * wide, order_count)

    def rows_of(wanted):
        placed = wanted[:, None] == lax.broadcasted_iota(jnp.int32, (1, order_count), 1)
        rows = lax.dot_general(
            placed.astype(jnp.bfloat16),
            parts,
            (((1,), (1,)), ((), ())),
            preferred_element_type=jnp.float32,
        )
        return rows.astype(jnp.bfloat16)

    sent = rows_of(order_table.reshape(-1))
    sent = sent.reshape(group_count, slot_count, 2 * pair_count, wide).transpose(0, 2, 1, 3)
    sent = sent.reshape(group_count, 2 * pair_count * slot_count, wide)
    received = lax.all_to_all(sent, "lat", split_axis=0, concat_axis=0, tiled=True)

    mode_parts = rows_of(mode_order).reshape(mode_count, 2, pair_count, wide)
    mode_odd = ((mode_degree - mode_order) % 2 == 1)[:, None, None]
    mode_side = jnp.where(mode_odd, mode_parts[:, 1], mode_parts[:, 0]).astype(jnp.float32)
    values = swapped_pair_sum(jnp.sum(mode_side * columns.T[:, :, None], axis=1))
    pieces, first = [], 0
    for reach, count in ((2, 3), (4, 2), (8, slot_count - 5)):
        piece, same = pl.pallas_call(
            functools.partial(basis_kernel, first=first, sources=group_count),
            in_specs=[in_vmem, in_hbm],
            out_specs=(in_hbm, in_vmem),
            out_shape=(
                pltpu.HBM((count, deg_count, pair_total), jnp.bfloat16),
                jax.ShapeDtypeStruct(values.shape, jnp.float32),
            ),
            scratch_shapes=[
                pltpu.VMEM((count, pair_total, deg_count), jnp.bfloat16),
                pltpu.VMEM((count, deg_count, pair_total), jnp.bfloat16),
                pltpu.SemaphoreType.DMA((count,)),
                pltpu.SemaphoreType.DMA((count,)),
            ],
            compiler_params=roomy,
            name="basis",
        )(values, pltpu.with_memory_space_constraint(basis, pltpu.HBM))
        pieces.append(pltpu.with_memory_space_constraint(piece, pltpu.HBM))
        first += count
        values = same + from_far(values, reach)
    plane = 16
    own = values.astype(jnp.bfloat16)
    for step in range(1, group_count // plane):
        route = [(i, (i + step * plane) % group_count) for i in range(group_count)]
        values = values + lax.ppermute(own, "lat", route).astype(jnp.float32)
    return pl.pallas_call(
        functools.partial(panel_kernel, scale=1.0 / (snap_count - 1)),
        in_specs=[in_smem, in_vmem, in_vmem] + [in_hbm] * len(pieces),
        out_specs=anywhere,
        out_shape=jax.ShapeDtypeStruct((1, slot_count, 2 * deg_count, 2 * mode_count), jnp.bfloat16),
        scratch_shapes=[
            pltpu.VMEM((slot_count, deg_count, pair_total), jnp.bfloat16),
            pltpu.VMEM((slot_count, 2 * deg_count, 2 * mode_count), jnp.bfloat16),
            pltpu.SemaphoreType.DMA((slot_count,)),
            pltpu.SemaphoreType.DMA((slot_count,)),
        ],
        compiler_params=roomy,
        name="panel",
    )(
        orders_by_slot,
        pltpu.with_memory_space_constraint(received.transpose(1, 0, 2), pltpu.VMEM),
        pltpu.with_memory_space_constraint(values, pltpu.VMEM),
        *pieces,
    )


def solution(mesh):
    placed = (P("field", None, None, "lat", None), P("lat", None, None), P(), P())
    return jax.shard_map(
        local, mesh=mesh, in_specs=placed, out_specs=P("field", "lat", None, None), check_vma=False
    )
```

```python
import functools
import math

import jax
import jax.numpy as jnp
import numpy as np
from jax import lax
from jax.experimental import pallas as pl
from jax.experimental.pallas import tpu as pltpu
from jax.sharding import PartitionSpec as P


def dft_table(lon_count, order_count):
    products = np.arange(lon_count // 2)[:, None] * np.arange(order_count)[None, :] % lon_count
    angles = products * (2.0 * math.pi / lon_count)
    return np.stack([np.cos(angles), -np.sin(angles)], axis=1).astype(jnp.bfloat16)


def from_far(block, reach):
    count = lax.axis_size("lat")
    return lax.ppermute(block, "lat", [(i, i ^ reach) for i in range(count)])


def stepped(block, reach):
    return block + from_far(block, reach)


def swapped_pair_sum(block):
    count = lax.axis_size("lat")
    both = ("lat", "field")
    near = [(2 * i + f, 2 * i + 1 - f) for i in range(count) for f in range(2)]
    far = [(2 * i + f, 2 * (i ^ 1) + 1 - f) for i in range(count) for f in range(2)]
    return lax.ppermute(block, both, near) + lax.ppermute(block, both, far)


def one_hot(condition):
    return condition.astype(jnp.float32).astype(jnp.bfloat16)


def column_kernel(orders_ref, modes_ref, basis_ref, out_ref, held_ref, total_ref, rows_ref, sems):
    group = lax.axis_index("lat")
    slots, pairs, degrees = held_ref.shape
    modes = modes_ref.shape[1]
    owned = [modes_ref[0:1, :] == orders_ref[s, group] for s in range(slots)]
    wanted = [jnp.max(row.astype(jnp.int32)) > 0 for row in owned]
    copies = [
        pltpu.make_async_copy(basis_ref.at[s], held_ref.at[s], sems.at[s]) for s in range(slots)
    ]
    for s in range(slots):
        pl.when(wanted[s])(copies[s].start)
    total_ref[...] = jnp.zeros_like(total_ref)
    here = lax.broadcasted_iota(jnp.int32, (degrees, modes), 0) == modes_ref[1:2, :]
    for s in range(slots):

        @pl.when(wanted[s])
        def _():
            pick = one_hot(here & owned[s])
            copies[s].wait()
            total_ref[...] += jnp.dot(held_ref[s], pick, preferred_element_type=jnp.float32)

    groups, halves, lanes = out_ref.shape
    share = pairs // groups
    blocks = [total_ref[pl.ds(j, groups, stride=share), :] for j in range(share)]
    blocks += [jnp.zeros_like(blocks[0])] * (halves * lanes // modes - share)
    per_half = lanes // modes
    for h in range(halves):
        half = jnp.concatenate(blocks[h * per_half : (h + 1) * per_half], axis=1)
        rows_ref[pl.ds(h, groups, stride=halves), :] = half
    out_ref[...] = rows_ref[...].astype(jnp.bfloat16).reshape(out_ref.shape)


def basis_kernel(
    values_ref, basis_ref, out_ref, same_ref, held_ref, rows_ref, sems, out_sems, *, first, sources
):
    same_ref[...] = values_ref[...]
    slots, _, pairs = out_ref.shape
    share = pairs // sources
    copies = [
        pltpu.make_async_copy(basis_ref.at[first + s], held_ref.at[s], sems.at[s])
        for s in range(slots)
    ]
    out_copies = [
        pltpu.make_async_copy(rows_ref.at[s], out_ref.at[s], out_sems.at[s]) for s in range(slots)
    ]
    for copy in copies:
        copy.start()
    row = lax.broadcasted_iota(jnp.int32, (pairs, pairs), 0)
    column = lax.broadcasted_iota(jnp.int32, (pairs, pairs), 1)
    place = one_hot(share * (column % sources) + column // sources == row)
    for s in range(slots):
        copies[s].wait()
        rows = lax.dot_general(
            held_ref[s], place, (((0,), (0,)), ((), ())), preferred_element_type=jnp.float32
        )
        rows_ref[s] = rows.astype(jnp.bfloat16)
        out_copies[s].start()
    for copy in out_copies:
        copy.wait()


def centered_columns(values):
    modes, wide = values.shape
    snaps = wide // 2
    values = values.astype(jnp.bfloat16).astype(jnp.float32)
    mode = lax.broadcasted_iota(jnp.int32, (modes, 2 * modes), 0)
    column = lax.broadcasted_iota(jnp.int32, (modes, 2 * modes), 1)
    block = jnp.zeros((snaps, 2 * modes), jnp.float32)
    for u in range(2):
        part = values[:, u * snaps : (u + 1) * snaps]
        part = (part - jnp.mean(part, axis=1, keepdims=True)).astype(jnp.bfloat16)
        block += lax.dot_general(
            part,
            one_hot(2 * mode + u == column),
            (((0,), (0,)), ((), ())),
            preferred_element_type=jnp.float32,
        )
    block = block.astype(jnp.bfloat16)
    blank = jnp.zeros_like(block)
    return jnp.concatenate(
        [jnp.concatenate([block, blank], axis=1), jnp.concatenate([blank, block], axis=1)], axis=0
    )


def panel_kernel(
    orders_ref,
    received_ref,
    values_ref,
    *refs,
    scale,
):
    *basis_refs, out_ref, held_ref, rows_ref, sems, out_sems = refs
    group = lax.axis_index("lat")
    slots, degrees, _ = held_ref.shape
    wide = received_ref.shape[2]
    parts = received_ref.shape[0] // slots
    sources = [ref.at[i] for ref in basis_refs for i in range(ref.shape[0])]
    copies = []
    for s in range(slots):
        copies.append(pltpu.make_async_copy(sources[s], held_ref.at[s], sems.at[s]))
        copies[s].start()
    out_copies = [
        pltpu.make_async_copy(rows_ref.at[s], out_ref.at[0, s], out_sems.at[s])
        for s in range(slots)
    ]
    centered = centered_columns(values_ref[...])
    degree = lax.broadcasted_iota(jnp.int32, (degrees, 1), 0)

    def of_both_parities(s):
        rows = [received_ref[k * slots + s] for k in range(parts)]
        sides = [
            jnp.concatenate(rows[: parts // 2], axis=0),
            jnp.concatenate(rows[parts // 2 :], axis=0),
        ]
        return jnp.dot(
            held_ref[s], jnp.concatenate(sides, axis=1), preferred_element_type=jnp.float32
        )

    def finish(s, both):
        order = orders_ref[s, group]
        odd = ((degree - order) & 1) == 1
        keep = (degree >= order) & (order >= 0)
        chosen = jnp.where(odd, both[:, wide:], both[:, :wide])
        coefficients = jnp.where(keep, chosen, 0.0).astype(jnp.bfloat16)
        products = jnp.dot(coefficients, centered, preferred_element_type=jnp.float32)
        rows_ref[s] = (products * scale).astype(jnp.bfloat16).reshape(rows_ref.shape[1:])

    begun = []
    bounds = list(range(0, slots, 2)) + [slots - 1, slots, slots]
    for start, end in zip(bounds[:-1], bounds[1:]):
        coming = range(start, end)
        for s in coming:
            copies[s].wait()
        new = [(s, of_both_parities(s)) for s in coming]
        for s, both in begun:
            finish(s, both)
        for s, _ in begun:
            out_copies[s].start()
        begun = new
    for copy in out_copies:
        copy.wait()


def local(fields_grid, basis, order_table, panel_modes):
    grid_one = fields_grid[0]
    snap_count, _, pair_count, lon_count = grid_one.shape
    group_count, slot_count = order_table.shape
    pair_total, deg_count = basis.shape[1], basis.shape[2]
    mode_count = panel_modes.shape[1]
    order_count = lon_count // 2
    wide = 2 * snap_count
    in_vmem = pl.BlockSpec(memory_space=pltpu.VMEM)
    in_smem = pl.BlockSpec(memory_space=pltpu.SMEM)
    anywhere = pl.BlockSpec(memory_space=pl.ANY)
    mode_order, mode_degree = panel_modes[0], panel_modes[1]
    orders_by_slot = order_table.T
    in_hbm = pl.BlockSpec(memory_space=pltpu.HBM)
    roomy = pltpu.CompilerParams(vmem_limit_bytes=32 << 20)

    columns = pl.pallas_call(
        column_kernel,
        in_specs=[in_smem, in_vmem, in_hbm],
        out_specs=in_vmem,
        out_shape=jax.ShapeDtypeStruct((group_count, 2, wide), jnp.bfloat16),
        scratch_shapes=[
            pltpu.VMEM((slot_count, pair_total, deg_count), jnp.bfloat16),
            pltpu.VMEM((pair_total, mode_count), jnp.float32),
            pltpu.VMEM((2 * group_count, wide), jnp.float32),
            pltpu.SemaphoreType.DMA((slot_count,)),
        ],
        name="columns",
    )(orders_by_slot, panel_modes, pltpu.with_memory_space_constraint(basis, pltpu.HBM))
    columns = lax.all_to_all(columns, "lat", split_axis=0, concat_axis=0, tiled=True)
    columns = jnp.sum(columns.astype(jnp.float32), axis=0).reshape(-1, mode_count)[:pair_count]

    table = jnp.asarray(dft_table(lon_count, order_count))
    products = [
        jnp.einsum("thjn,nrm->hjrtm", half, table, preferred_element_type=jnp.float32)
        for half in (grid_one[..., :order_count], grid_one[..., order_count:])
    ]
    sign = 1.0 - 2.0 * (lax.iota(jnp.int32, order_count) % 2).astype(jnp.float32)
    fourier = (products[0] + products[1] * sign) * (1.0 / math.sqrt(lon_count))
    parts = jnp.stack([fourier[0] + fourier[1], fourier[0] - fourier[1]]).astype(jnp.bfloat16)
    parts = parts.reshape(2 * pair_count * wide, order_count)

    def rows_of(wanted):
        placed = wanted[:, None] == lax.broadcasted_iota(jnp.int32, (1, order_count), 1)
        rows = lax.dot_general(
            placed.astype(jnp.bfloat16),
            parts,
            (((1,), (1,)), ((), ())),
            preferred_element_type=jnp.float32,
        )
        return rows.astype(jnp.bfloat16)

    sent = rows_of(order_table.reshape(-1))
    sent = sent.reshape(group_count, slot_count, 2 * pair_count, wide).transpose(0, 2, 1, 3)
    sent = sent.reshape(group_count, 2 * pair_count * slot_count, wide)
    received = lax.all_to_all(sent, "lat", split_axis=0, concat_axis=0, tiled=True)

    mode_parts = rows_of(mode_order).reshape(mode_count, 2, pair_count, wide)
    mode_odd = ((mode_degree - mode_order) % 2 == 1)[:, None, None]
    mode_side = jnp.where(mode_odd, mode_parts[:, 1], mode_parts[:, 0]).astype(jnp.float32)
    values = swapped_pair_sum(jnp.sum(mode_side * columns.T[:, :, None], axis=1))
    pieces, first = [], 0
    for reach, count in ((2, 3), (4, 2), (8, slot_count - 5)):
        piece, same = pl.pallas_call(
            functools.partial(basis_kernel, first=first, sources=group_count),
            in_specs=[in_vmem, in_hbm],
            out_specs=(in_hbm, in_vmem),
            out_shape=(
                pltpu.HBM((count, deg_count, pair_total), jnp.bfloat16),
                jax.ShapeDtypeStruct(values.shape, jnp.float32),
            ),
            scratch_shapes=[
                pltpu.VMEM((count, pair_total, deg_count), jnp.bfloat16),
                pltpu.VMEM((count, deg_count, pair_total), jnp.bfloat16),
                pltpu.SemaphoreType.DMA((count,)),
                pltpu.SemaphoreType.DMA((count,)),
            ],
            compiler_params=roomy,
            name="basis",
        )(values, pltpu.with_memory_space_constraint(basis, pltpu.HBM))
        pieces.append(pltpu.with_memory_space_constraint(piece, pltpu.HBM))
        first += count
        values = same + from_far(values, reach)
    plane = 16
    own = values.astype(jnp.bfloat16)
    for step in range(1, group_count // plane):
        values = values + from_far(own, step * plane).astype(jnp.float32)
    return pl.pallas_call(
        functools.partial(panel_kernel, scale=1.0 / (snap_count - 1)),
        in_specs=[in_smem, in_vmem, in_vmem] + [in_hbm] * len(pieces),
        out_specs=anywhere,
        out_shape=jax.ShapeDtypeStruct((1, slot_count, 2 * deg_count, 2 * mode_count), jnp.bfloat16),
        scratch_shapes=[
            pltpu.VMEM((slot_count, deg_count, pair_total), jnp.bfloat16),
            pltpu.VMEM((slot_count, 2 * deg_count, 2 * mode_count), jnp.bfloat16),
            pltpu.SemaphoreType.DMA((slot_count,)),
            pltpu.SemaphoreType.DMA((slot_count,)),
        ],
        compiler_params=roomy,
        name="panel",
    )(
        orders_by_slot,
        pltpu.with_memory_space_constraint(received.transpose(1, 0, 2), pltpu.VMEM),
        pltpu.with_memory_space_constraint(values, pltpu.VMEM),
        *pieces,
    )


def solution(mesh):
    placed = (P("field", None, None, "lat", None), P("lat", None, None), P(), P())
    return jax.shard_map(
        local, mesh=mesh, in_specs=placed, out_specs=P("field", "lat", None, None), check_vma=False
    )
```
